512 devices in a mesh: doc: 32 (over z, x), cent: 16 (over y, core).
Axes of the slice: x: 4, y: 8, z: 8, core: 2. Of those that a mesh axis runs over, the one named last changes fastest.
Arguments:
- rows: bfloat16 [65536, 1024], P('doc'), may hold values from -30 to 30
- centroids: bfloat16 [8192, 1024], P('cent'), may hold values from -16 to 16
Outputs:
- new_centroids: float32 [8192, 1024], P(('cent', 'doc'))
The draws below stay inside these ranges and needn't reach their ends.
All inputs are finite; a program needn't handle non-finite values.
Results may differ from the reference program's by a relative error of at most 0.0009.
Values sent between devices are 32-bit elements; how exact they have to be, the bound alone decides.
A program may use at most 64 MiB of HBM per device.

```python
import math
import jax
import jax.numpy as jnp
from jax import lax

D = 1024
K = 8192
ROWS_DEV = 2048
ROWS = 65536


def drawn_pairs():
    targets = jnp.array([120.0, 250.0, 400.0, 120.0, 250.0, 400.0], jnp.float32)
    centre_index = jnp.arange(6) * (K // 6)
    row_index = jnp.arange(6) * (ROWS // 6) + 1
    return (targets, centre_index, row_index)


def centroid_table(key):
    first, second = jax.random.split(jax.random.fold_in(key, 3), 2)
    base = jnp.clip(jax.random.normal(first, (K, D), jnp.float32), -6.0, 6.0)
    scales = jnp.exp(jax.random.uniform(second, (K, 1), jnp.float32, math.log(0.4), math.log(2.5)))
    table = base * scales
    targets, centre_index, row_index = drawn_pairs()
    magnitude = jnp.sqrt(targets * 0.6 / math.sqrt(D))
    signs = jnp.where(base[centre_index] >= 0.0, 1.0, -1.0)
    planted = magnitude[:, None] * signs
    table = table.at[centre_index].set(planted)
    table = table.at[centre_index + 1].set((1.0 - 2.0 / targets)[:, None] * planted + 0.05 * base[centre_index + 1])
    return table


def draw_centroids(key, part):
    return centroid_table(key).astype(jnp.bfloat16)


def draw_rows(key, part):
    first, second = jax.random.split(jax.random.fold_in(key, 7), 2)
    scales = jnp.exp(jax.random.uniform(second, (ROWS, 1), jnp.float32, math.log(0.3), math.log(3.0)))
    values = scales * jnp.clip(jax.random.normal(first, (ROWS, D), jnp.float32), -6.0, 6.0)
    targets, centre_index, row_index = drawn_pairs()
    table = centroid_table(key).astype(jnp.bfloat16).astype(jnp.float32)
    values = values.at[row_index].set(table[centre_index])
    return values.astype(jnp.bfloat16)


def setup_inputs(seed: int = 0) -> dict:
    key_of = jax.random.split(jax.random.key(seed), 3)
    rows = draw_rows(jax.random.fold_in(key_of[2], 71), 0)
    centroids = draw_centroids(jax.random.fold_in(key_of[2], 71), 0)
    return dict(rows=rows, centroids=centroids)


def reference(rows, centroids):
    scale = 1.0 / (0.6 * math.sqrt(D))
    blocks = rows.reshape(ROWS // ROWS_DEV, ROWS_DEV, D)

    def step(carry, block):
        sums, totals = carry
        logits = jnp.dot(block, centroids.T, preferred_element_type=jnp.float32) * scale
        top = lax.optimization_barrier(jnp.max(logits, axis=1))
        lse = top + jnp.log(lax.optimization_barrier(jnp.sum(jnp.exp(logits - top[:, None]), axis=1)))
        resp = jnp.exp(logits - lse[:, None]).astype(jnp.bfloat16)
        sums = sums + jnp.dot(resp.T, block, preferred_element_type=jnp.float32)
        totals = totals + lax.optimization_barrier(jnp.sum(resp.astype(jnp.float32), axis=0))
        return ((sums, totals), None)
    init = (jnp.zeros((K, D), jnp.float32), jnp.zeros((K,), jnp.float32))
    (sums, totals), unused = lax.scan(step, init, blocks)
    return (sums + centroids.astype(jnp.float32)) / (totals[:, None] + 1.0)
```

```python
import math

import jax
import jax.numpy as jnp
from jax import lax
from jax.sharding import PartitionSpec as P


def on_device(rows, centroids):
    scale = 1.0 / (0.6 * math.sqrt(rows.shape[1]))
    logits = jnp.einsum("kd,rd->kr", centroids, rows, preferred_element_type=jnp.float32) * scale
    top = jnp.max(logits, axis=0)
    part = jnp.sum(jnp.exp(logits - top[None, :]), axis=0)
    stats = lax.all_gather(top + jnp.log(part), "cent")
    highest = jnp.max(stats, axis=0)
    lse = highest + jnp.log(jnp.sum(jnp.exp(stats - highest[None, :]), axis=0))
    resp = jnp.exp(logits - lse[None, :]).astype(jnp.bfloat16)
    sums = jnp.einsum("kr,rd->kd", resp, rows, preferred_element_type=jnp.float32)
    totals = jnp.sum(resp, axis=1, dtype=jnp.float32)
    both = jnp.concatenate([sums, jnp.broadcast_to(totals[:, None], (sums.shape[0], 128))], axis=1)
    mine = lax.psum_scatter(both, "doc", scatter_dimension=0, tiled=True)
    share = mine.shape[0]
    start = lax.axis_index("doc") * share
    own_rows = lax.dynamic_slice_in_dim(centroids, start, share, 0).astype(jnp.float32)
    width = rows.shape[1]
    return (mine[:, :width] + own_rows) / (mine[:, width : width + 1] + 1.0)


def solution(mesh):
    return jax.shard_map(
        on_device,
        mesh=mesh,
        in_specs=(P("doc", None), P("cent", None)),
        out_specs=P(("cent", "doc"), None),
        check_vma=False,
    )
```

```python
import functools
import math

import jax
import jax.numpy as jnp
from jax import lax
from jax.experimental import pallas as pl
from jax.experimental.pallas import tpu as pltpu
from jax.sharding import PartitionSpec as P

MESH = pl.DeviceIdType.MESH
F32 = jnp.float32
NZ, NX = 8, 4
LANES = 128
BLOCKS = ((0, 256, True), (256, 256, False), (512, 256, True), (768, 256, False))


def ring(me, n, device, data, half_in, full_in, send_sems, recv_sems, sent):
    h = data.shape[1] // 2
    last = n // 2
    copies = [None, None]
    for step in range(1, last + 1):
        for way, sign in enumerate((1, -1)):
            chunk = data.at[lax.rem(me + sign * (last + 1 - step) + n, n)]
            half = pl.ds(way * h, h)
            if step == 1:
                source, target = chunk.at[half], half_in.at[way]
            else:
                copies[way].wait_recv()
                if step == 2:
                    chunk[half] += half_in[way]
                else:
                    chunk[...] += full_in[way, step - 3]
                source, target = chunk, full_in.at[way, step - 2]
            copies[way] = pltpu.make_async_remote_copy(
                src_ref=source,
                dst_ref=target,
                send_sem=send_sems.at[way, step - 1],
                recv_sem=recv_sems.at[way, step - 1],
                device_id=device(lax.rem(me + sign + n, n)),
                device_id_type=MESH,
            )
            copies[way].start()
            sent.append(copies[way])
        yield
    own = data.at[me]
    for way in range(2):
        copies[way].wait_recv()
        own[...] += full_in[way, last - 2]


def kernel(scale, ncent, *refs):
    rows_hbm, cent_ref, out_ref, x_v, p_v, resp_v, top_v, stat_v, tot_v = refs[:9]
    in_sems, stat_send, stat_recv = refs[9:12]
    block_refs = [refs[12 + 9 * b : 21 + 9 * b] for b in range(len(BLOCKS))]
    rows, step = x_v.shape[0], 512
    nsteps = rows // step
    doc, cent = lax.axis_index("doc"), lax.axis_index("cent")
    z, x = doc // NX, lax.rem(doc, NX)

    def chunk_in(i):
        part = pl.ds(pl.multiple_of(i * step, step), step)
        return pltpu.make_async_copy(rows_hbm.at[part], x_v.at[part], in_sems.at[i])

    for i in range(nsteps):
        chunk_in(i).start()

    def at_z(k):
        return {"doc": k * NX + x}

    def at_x(k):
        return {"doc": z * NX + k}

    barrier = pltpu.get_barrier_semaphore()
    near = [at_z(lax.rem(z + 1, NZ)), at_z(lax.rem(z + NZ - 1, NZ))]
    near += [at_x(lax.rem(x + 1, NX)), at_x(lax.rem(x + NX - 1, NX))]
    near += [{"cent": lax.rem(cent + k, ncent)} for k in range(1, ncent)]
    for other in near:
        pl.semaphore_signal(barrier, inc=1, device_id=other, device_id_type=MESH)

    def logits_step(i, carry):
        chunk_in(i).wait()
        part = pl.ds(pl.multiple_of(i * step, step), step)
        logits = lax.dot_general(
            cent_ref[...], x_v[part, :], (((1,), (1,)), ((), ())), preferred_element_type=F32
        ) * scale
        top = jnp.max(logits, axis=0, keepdims=True)
        p = jnp.exp(logits - top)
        p_v[:, part] = p
        top_v[:, part] = top
        stat_v[0, :, part] = top + jnp.log(jnp.sum(p, axis=0, keepdims=True))
        return carry

    lax.fori_loop(0, nsteps, logits_step, 0)
    pl.semaphore_wait(barrier, len(near))

    stat_copies = []
    for k in range(1, ncent):
        stat_copies.append(
            pltpu.make_async_remote_copy(
                src_ref=stat_v.at[0],
                dst_ref=stat_v.at[k],
                send_sem=stat_send.at[k],
                recv_sem=stat_recv.at[k],
                device_id={"cent": lax.rem(cent + k, ncent)},
                device_id_type=MESH,
            )
        )
        stat_copies[-1].start()
    for copy in stat_copies:
        copy.wait_recv()

    stats = stat_v[...]
    highest = jnp.max(stats, axis=0)
    lse = highest + jnp.log(jnp.sum(jnp.exp(stats - highest[None]), axis=0))
    top_v[...] = jnp.exp(top_v[...] - lse)
    tot_v[...] = jnp.zeros_like(tot_v)

    def resp_step(i, carry):
        part = pl.ds(pl.multiple_of(i * step, step), step)
        resp = (p_v[:, part] * top_v[:, part]).astype(jnp.bfloat16)
        resp_v[:, part] = resp
        wide = resp.astype(F32)
        total = tot_v[...]
        for j in range(step // LANES):
            total += wide[:, j * LANES : (j + 1) * LANES]
        tot_v[...] = total
        return carry

    lax.fori_loop(0, nsteps, resp_step, 0)

    sent = []
    active = []
    share = out_ref.shape[0]

    def run(b):
        _, _, x_first = BLOCKS[b]
        data, h1, f1, s1, r1, h2, f2, s2, r2 = block_refs[b]
        first = (x, NX, at_x) if x_first else (z, NZ, at_z)
        second = (z, NZ, at_z) if x_first else (x, NX, at_x)
        yield from ring(*first, data, h1, f1, s1, r1, sent)
        yield from ring(*second, data.at[first[0]], h2, f2, s2, r2, sent)

    def put(data, x_first, first, width, value):
        for k in range(NZ):
            tile = value[k * NX * share : (k + 1) * NX * share].reshape(NX, share, width)
            if x_first:
                data[:, k, :, first : first + width] = tile
            else:
                data[k, :, :, first : first + width] = tile

    for b, (start, width, x_first) in enumerate(BLOCKS):
        data = block_refs[b][0]
        value = jnp.dot(resp_v[...], x_v[:, start : start + width], preferred_element_type=F32)
        put(data, x_first, 0, width, value)
        if b == 0:
            put(data, x_first, width, LANES, tot_v[...])
        active.append(run(b))
        next(active[-1])
    while active:
        for gen in list(active):
            if next(gen, None) is None and gen.gi_frame is None:
                active.remove(gen)

    own = cent_ref[pl.ds(pl.multiple_of(doc * share, share), share), :].astype(F32)
    total = None
    for b, (start, width, x_first) in enumerate(BLOCKS):
        value = block_refs[b][0][(x, z) if x_first else (z, x)]
        if b == 0:
            total = jnp.sum(value[:, width:], axis=1, keepdims=True) + 1.0
        out_ref[:, start : start + width] = (value[:, :width] + own[:, start : start + width]) / total
    for copy in stat_copies + sent:
        copy.wait_send()


def on_device(rows, centroids):
    nrows, d = rows.shape
    local = centroids.shape[0]
    ncent = lax.axis_size("cent")
    share = local // (NZ * NX)
    scale = 1.0 / (0.6 * math.sqrt(d))
    dma = pltpu.SemaphoreType.DMA
    scratch = [
        pltpu.VMEM((nrows, d), jnp.bfloat16),
        pltpu.VMEM((local, nrows), F32),
        pltpu.VMEM((local, nrows), jnp.bfloat16),
        pltpu.VMEM((1, nrows), F32),
        pltpu.VMEM((ncent, 1, nrows), F32),
        pltpu.VMEM((local, LANES), F32),
        dma((nrows // 512,)),
        dma((ncent,)),
        dma((ncent,)),
    ]
    for b, (_, width, x_first) in enumerate(BLOCKS):
        w = width + (LANES if b == 0 else 0)
        n1, n2 = (NX, NZ) if x_first else (NZ, NX)
        scratch += [
            pltpu.VMEM((n1, n2, share, w), F32),
            pltpu.VMEM((2, n2 // 2, share, w), F32),
            pltpu.VMEM((2, n1 // 2 - 1, n2, share, w), F32),
            dma((2, n1 // 2)),
            dma((2, n1 // 2)),
            pltpu.VMEM((2, share // 2, w), F32),
            pltpu.VMEM((2, n2 // 2 - 1, share, w), F32),
            dma((2, n2 // 2)),
            dma((2, n2 // 2)),
        ]
    return pl.pallas_call(
        functools.partial(kernel, scale, ncent),
        out_shape=jax.ShapeDtypeStruct((share, d), F32),
        in_specs=[pl.BlockSpec(memory_space=pl.ANY), pl.BlockSpec(memory_space=pltpu.VMEM)],
        out_specs=pl.BlockSpec(memory_space=pltpu.VMEM),
        scratch_shapes=scratch,
        compiler_params=pltpu.CompilerParams(collective_id=0, has_side_effects=True),
    )(rows, centroids)


def solution(mesh):
    return jax.shard_map(
        on_device,
        mesh=mesh,
        in_specs=(P("doc", None), P("cent", None)),
        out_specs=P(("cent", "doc"), None),
        check_vma=False,
    )
```

```python
import functools
import math

import jax
import jax.numpy as jnp
from jax import lax
from jax.experimental import pallas as pl
from jax.experimental.pallas import tpu as pltpu
from jax.sharding import PartitionSpec as P

MESH = pl.DeviceIdType.MESH
F32 = jnp.float32
NZ, NX = 8, 4
LANES = 128
BLOCKS = ((0, 128, True), (128, 256, False), (384, 256, True), (640, 128, True), (768, 256, False))
ORDER = (1, 0, 4, 2, 3, 1, 4, 0, 1, 2, 4, 3, 0, 1, 2, 4, 3, 1, 0, 2, 4, 3)


def scatter(mode, me, n, device, data, half_in, full_in, send_sems, recv_sems, sent):
    h = data.shape[1] // 2
    last = n // 2

    def chunk_at(way, k):
        return data.at[lax.rem(me + (k if way == 0 else n - k), n)]

    def send(way, slot, source, k):
        copy = pltpu.make_async_remote_copy(
            src_ref=source,
            dst_ref=half_in.at[way] if slot == 0 else full_in.at[way, slot - 1],
            send_sem=send_sems.at[way, slot],
            recv_sem=recv_sems.at[way, slot],
            device_id=device(lax.rem(me + (k if way == 0 else n - k), n)),
            device_id_type=MESH,
        )
        copy.start()
        sent.append(copy)
        return copy

    halves = [pl.ds(0, h), pl.ds(h, h)]
    both = (0, 1)
    own = data.at[me]
    if mode == "direct":
        far = [send(w, 0, chunk_at(w, last).at[halves[w]], last) for w in both]
        near = [send(w, 1, chunk_at(w, 1), 1) for w in both]
        yield
        for w in both:
            near[w].wait_recv()
            far[w].wait_recv()
        own[...] += full_in[0, 0] + full_in[1, 0]
        for w in both:
            own[halves[w]] += half_in[w]
    elif mode == "hub":
        far = [send(w, 0, chunk_at(w, 4).at[halves[w]], 2) for w in both]
        near = [send(w, 1, chunk_at(w, 3), 1) for w in both]
        yield
        for w in both:
            near[w].wait_recv()
            far[w].wait_recv()
            hub = chunk_at(w, 2)
            hub[...] += full_in[w, 0]
            hub[halves[w]] += half_in[w]
            far[w] = send(w, 2, hub, 2)
        near = [send(w, 3, chunk_at(w, 1), 1) for w in both]
        yield
        for w in both:
            near[w].wait_recv()
            far[w].wait_recv()
        own[...] += (full_in[0, 1] + full_in[0, 2]) + (full_in[1, 1] + full_in[1, 2])
    else:
        copies = [None, None]
        for slot in range(last):
            for w in both:
                chunk = chunk_at(w, last - slot)
                if slot == 0:
                    copies[w] = send(w, 0, chunk.at[halves[w]], 1)
                    continue
                copies[w].wait_recv()
                if slot == 1:
                    chunk[halves[w]] += half_in[w]
                else:
                    chunk[...] += full_in[w, slot - 2]
                copies[w] = send(w, slot, chunk, 1)
            yield
        for w in both:
            copies[w].wait_recv()
        own[...] += full_in[0, last - 2] + full_in[1, last - 2]


def kernel(scale, ncent, *refs):
    rows_hbm, cent_ref, out_ref, x_v, p_v, resp_v, top_v, stat_v, pair_v, tot_v = refs[:10]
    in_sems, stat_send, stat_recv = refs[10:13]
    block_refs = [refs[13 + 9 * b : 22 + 9 * b] for b in range(len(BLOCKS))]
    rows, step = x_v.shape[0], 512
    nsteps = rows // step
    doc, cent = lax.axis_index("doc"), lax.axis_index("cent")
    z, x = doc // NX, lax.rem(doc, NX)

    def chunk_in(i):
        part = pl.ds(pl.multiple_of(i * step, step), step)
        return pltpu.make_async_copy(rows_hbm.at[part], x_v.at[part], in_sems.at[i])

    for i in range(nsteps):
        chunk_in(i).start()

    def at_z(k):
        return {"doc": k * NX + x}

    def at_x(k):
        return {"doc": z * NX + k}

    barrier = pltpu.get_barrier_semaphore()
    near = [at_z(lax.rem(z + k, NZ)) for k in (1, 2, NZ - 2, NZ - 1)]
    near += [at_x(lax.rem(x + k, NX)) for k in range(1, NX)]
    near += [{"cent": lax.rem(cent + k, ncent)} for k in range(2, ncent, 2)]
    partner = {"cent": cent + 1 - 2 * lax.rem(cent, 2)}
    near.append(partner)
    for other in near:
        pl.semaphore_signal(barrier, inc=1, device_id=other, device_id_type=MESH)

    def logits_step(i, carry):
        chunk_in(i).wait()
        part = pl.ds(pl.multiple_of(i * step, step), step)
        logits = lax.dot_general(
            cent_ref[...], x_v[part, :], (((1,), (1,)), ((), ())), preferred_element_type=F32
        ) * scale
        top = jnp.max(logits, axis=0, keepdims=True)
        p = jnp.exp(logits - top)
        p_v[:, part] = p
        top_v[:, part] = top
        stat_v[0, :, part] = top + jnp.log(jnp.sum(p, axis=0, keepdims=True))
        return carry

    lax.fori_loop(0, nsteps, logits_step, 0)
    pl.semaphore_wait(barrier, len(near))

    def log_sum_exp(values):
        highest = jnp.max(values, axis=0)
        return highest + jnp.log(jnp.sum(jnp.exp(values - highest[None]), axis=0))

    chips = ncent // 2
    stat_copies = []
    for k in sorted(range(1, chips), key=lambda k: -min(k, chips - k)):
        stat_copies.append(
            pltpu.make_async_remote_copy(
                src_ref=stat_v.at[0],
                dst_ref=stat_v.at[k],
                send_sem=stat_send.at[k],
                recv_sem=stat_recv.at[k],
                device_id={"cent": lax.rem(cent + 2 * k, ncent)},
                device_id_type=MESH,
            )
        )
        stat_copies[-1].start()
    for copy in stat_copies:
        copy.wait_recv()
    pair_v[0] = log_sum_exp(stat_v[...])
    swap = pltpu.make_async_remote_copy(
        src_ref=pair_v.at[0],
        dst_ref=pair_v.at[1],
        send_sem=stat_send.at[0],
        recv_sem=stat_recv.at[0],
        device_id=partner,
        device_id_type=MESH,
    )
    swap.start()
    stat_copies.append(swap)
    swap.wait_recv()
    top_v[...] = jnp.exp(top_v[...] - log_sum_exp(pair_v[...]))
    tot_v[...] = jnp.zeros_like(tot_v)

    def resp_step(i, carry):
        part = pl.ds(pl.multiple_of(i * step, step), step)
        resp = (p_v[:, part] * top_v[:, part]).astype(jnp.bfloat16)
        resp_v[:, part] = resp
        wide = resp.astype(F32)
        total = tot_v[...]
        for j in range(step // LANES):
            total += wide[:, j * LANES : (j + 1) * LANES]
        tot_v[...] = total
        return carry

    lax.fori_loop(0, nsteps, resp_step, 0)

    sent = []
    active = []
    share = out_ref.shape[0]

    def run(b):
        _, _, x_first = BLOCKS[b]
        data, h1, f1, s1, r1, h2, f2, s2, r2 = block_refs[b]
        first = (x, NX, at_x) if x_first else (z, NZ, at_z)
        second = (z, NZ, at_z) if x_first else (x, NX, at_x)
        yield from scatter("ring", *first, data, h1, f1, s1, r1, sent)
        mode = "hub" if x_first else "direct"
        yield from scatter(mode, *second, data.at[first[0]], h2, f2, s2, r2, sent)

    def put(data, x_first, first, width, value):
        for k in range(NZ):
            tile = value[k * NX * share : (k + 1) * NX * share].reshape(NX, share, width)
            if x_first:
                data[:, k, :, first : first + width] = tile
            else:
                data[k, :, :, first : first + width] = tile

    for b, (start, width, x_first) in enumerate(BLOCKS):
        data = block_refs[b][0]
        value = jnp.dot(resp_v[...], x_v[:, start : start + width], preferred_element_type=F32)
        put(data, x_first, 0, width, value)
        if b == 0:
            put(data, x_first, width, LANES, tot_v[...])
        active.append(run(b))
        next(active[-1])
    for b in ORDER:
        next(active[b], None)
    assert all(gen.gi_frame is None for gen in active)

    own = cent_ref[pl.ds(pl.multiple_of(doc * share, share), share), :].astype(F32)
    total = None
    for b, (start, width, x_first) in enumerate(BLOCKS):
        value = block_refs[b][0][(x, z) if x_first else (z, x)]
        if b == 0:
            total = jnp.sum(value[:, width:], axis=1, keepdims=True) + 1.0
        out_ref[:, start : start + width] = (value[:, :width] + own[:, start : start + width]) / total
    for copy in stat_copies + sent:
        copy.wait_send()


def on_device(rows, centroids):
    nrows, d = rows.shape
    local = centroids.shape[0]
    ncent = lax.axis_size("cent")
    share = local // (NZ * NX)
    scale = 1.0 / (0.6 * math.sqrt(d))
    dma = pltpu.SemaphoreType.DMA
    scratch = [
        pltpu.VMEM((nrows, d), jnp.bfloat16),
        pltpu.VMEM((local, nrows), F32),
        pltpu.VMEM((local, nrows), jnp.bfloat16),
        pltpu.VMEM((1, nrows), F32),
        pltpu.VMEM((ncent // 2, 1, nrows), F32),
        pltpu.VMEM((2, 1, nrows), F32),
        pltpu.VMEM((local, LANES), F32),
        dma((nrows // 512,)),
        dma((ncent // 2,)),
        dma((ncent // 2,)),
    ]
    for b, (_, width, x_first) in enumerate(BLOCKS):
        w = width + (LANES if b == 0 else 0)
        n1, n2 = (NX, NZ) if x_first else (NZ, NX)
        scratch += [
            pltpu.VMEM((n1, n2, share, w), F32),
            pltpu.VMEM((2, n2 // 2, share, w), F32),
            pltpu.VMEM((2, n1 // 2 - 1, n2, share, w), F32),
            dma((2, n1 // 2)),
            dma((2, n1 // 2)),
            pltpu.VMEM((2, share // 2, w), F32),
            pltpu.VMEM((2, n2 // 2 - 1, share, w), F32),
            dma((2, n2 // 2)),
            dma((2, n2 // 2)),
        ]
    return pl.pallas_call(
        functools.partial(kernel, scale, ncent),
        out_shape=jax.ShapeDtypeStruct((share, d), F32),
        in_specs=[pl.BlockSpec(memory_space=pl.ANY), pl.BlockSpec(memory_space=pltpu.VMEM)],
        out_specs=pl.BlockSpec(memory_space=pltpu.VMEM),
        scratch_shapes=scratch,
        compiler_params=pltpu.CompilerParams(collective_id=0, has_side_effects=True),
    )(rows, centroids)


def solution(mesh):
    return jax.shard_map(
        on_device,
        mesh=mesh,
        in_specs=(P("doc", None), P("cent", None)),
        out_specs=P(("cent", "doc"), None),
        check_vma=False,
    )
```

```python
import functools
import math

import jax
import jax.numpy as jnp
from jax import lax
from jax.experimental import pallas as pl
from jax.experimental.pallas import tpu as pltpu
from jax.sharding import PartitionSpec as P

MESH = pl.DeviceIdType.MESH
F32 = jnp.float32
NZ, NX = 8, 4
LANES = 128
BLOCKS = ((0, 256, True), (256, 256, False), (512, 256, True), (768, 256, False))
ORDER = (1, 0, 3, 2, 4, 1, 3, 0, 1, 2, 3, 0, 1, 2, 3, 1, 0, 2, 3, 4)


def scatter(mode, me, n, device, data, half_in, full_in, send_sems, recv_sems, sent):
    h = data.shape[1] // 2
    last = n // 2

    def chunk_at(way, k):
        return data.at[lax.rem(me + (k if way == 0 else n - k), n)]

    def send(way, slot, source, k):
        copy = pltpu.make_async_remote_copy(
            src_ref=source,
            dst_ref=half_in.at[way] if slot == 0 else full_in.at[way, slot - 1],
            send_sem=send_sems.at[way, slot],
            recv_sem=recv_sems.at[way, slot],
            device_id=device(lax.rem(me + (k if way == 0 else n - k), n)),
            device_id_type=MESH,
        )
        copy.start()
        sent.append(copy)
        return copy

    halves = [pl.ds(0, h), pl.ds(h, h)]
    both = (0, 1)
    own = data.at[me]
    if mode == "direct":
        far = [send(w, 0, chunk_at(w, last).at[halves[w]], last) for w in both]
        near = [send(w, 1, chunk_at(w, 1), 1) for w in both]
        yield
        for w in both:
            near[w].wait_recv()
            far[w].wait_recv()
        own[...] += full_in[0, 0] + full_in[1, 0]
        for w in both:
            own[halves[w]] += half_in[w]
    elif mode == "hub":
        far = [send(w, 0, chunk_at(w, 4).at[halves[w]], 2) for w in both]
        near = [send(w, 1, chunk_at(w, 3), 1) for w in both]
        yield
        for w in both:
            near[w].wait_recv()
            far[w].wait_recv()
            hub = chunk_at(w, 2)
            hub[...] += full_in[w, 0]
            hub[halves[w]] += half_in[w]
            far[w] = send(w, 2, hub, 2)
        near = [send(w, 3, chunk_at(w, 1), 1) for w in both]
        yield
        for w in both:
            near[w].wait_recv()
            far[w].wait_recv()
        own[...] += (full_in[0, 1] + full_in[0, 2]) + (full_in[1, 1] + full_in[1, 2])
    else:
        copies = [None, None]
        for slot in range(last):
            for w in both:
                chunk = chunk_at(w, last - slot)
                if slot == 0:
                    copies[w] = send(w, 0, chunk.at[halves[w]], 1)
                    continue
                copies[w].wait_recv()
                if slot == 1:
                    chunk[halves[w]] += half_in[w]
                else:
                    chunk[...] += full_in[w, slot - 2]
                copies[w] = send(w, slot, chunk, 1)
            yield
        for w in both:
            copies[w].wait_recv()
        own[...] += full_in[0, last - 2] + full_in[1, last - 2]


def kernel(scale, ncent, *refs):
    rows_hbm, cent_ref, out_ref, x_v, p_v, resp_v, top_v, stat_v, pair_v, tot_v = refs[:10]
    own_tot_v, x_tot_v, z_tot_v, x_send, x_recv, z_send, z_recv = refs[13:20]
    in_sems, stat_send, stat_recv = refs[10:13]
    block_refs = [refs[20 + 9 * b : 29 + 9 * b] for b in range(len(BLOCKS))]
    rows, step = x_v.shape[0], 512
    nsteps = rows // step
    doc, cent = lax.axis_index("doc"), lax.axis_index("cent")
    z, x = doc // NX, lax.rem(doc, NX)

    def chunk_in(i):
        part = pl.ds(pl.multiple_of(i * step, step), step)
        return pltpu.make_async_copy(rows_hbm.at[part], x_v.at[part], in_sems.at[i])

    for i in range(nsteps):
        chunk_in(i).start()

    def at_z(k):
        return {"doc": k * NX + x}

    def at_x(k):
        return {"doc": z * NX + k}

    barrier = pltpu.get_barrier_semaphore()
    near = [at_z(lax.rem(z + k, NZ)) for k in range(1, NZ)]
    near += [at_x(lax.rem(x + k, NX)) for k in range(1, NX)]
    near += [{"cent": lax.rem(cent + k, ncent)} for k in range(2, ncent, 2)]
    partner = {"cent": cent + 1 - 2 * lax.rem(cent, 2)}
    near.append(partner)
    for other in near:
        pl.semaphore_signal(barrier, inc=1, device_id=other, device_id_type=MESH)

    def logits_step(i, carry):
        chunk_in(i).wait()
        part = pl.ds(pl.multiple_of(i * step, step), step)
        logits = lax.dot_general(
            cent_ref[...], x_v[part, :], (((1,), (1,)), ((), ())), preferred_element_type=F32
        ) * scale
        top = jnp.max(logits, axis=0, keepdims=True)
        p = jnp.exp(logits - top)
        p_v[:, part] = p
        top_v[:, part] = top
        lse = top + jnp.log(jnp.sum(p, axis=0, keepdims=True))
        stat_v[0, :, part] = lse
        return carry

    lax.fori_loop(0, nsteps, logits_step, 0)
    pl.semaphore_wait(barrier, len(near))

    def log_sum_exp(values):
        highest = jnp.max(values, axis=0)
        return highest + jnp.log(jnp.sum(jnp.exp(values - highest[None]), axis=0))

    chips = ncent // 2
    stat_copies = []
    for k in sorted(range(1, chips), key=lambda k: -min(k, chips - k)):
        stat_copies.append(
            pltpu.make_async_remote_copy(
                src_ref=stat_v.at[0],
                dst_ref=stat_v.at[k],
                send_sem=stat_send.at[k],
                recv_sem=stat_recv.at[k],
                device_id={"cent": lax.rem(cent + 2 * k, ncent)},
                device_id_type=MESH,
            )
        )
        stat_copies[-1].start()
    for copy in stat_copies:
        copy.wait_recv()
    pair_v[0] = log_sum_exp(stat_v[...])
    swap = pltpu.make_async_remote_copy(
        src_ref=pair_v.at[0],
        dst_ref=pair_v.at[1],
        send_sem=stat_send.at[0],
        recv_sem=stat_recv.at[0],
        device_id=partner,
        device_id_type=MESH,
    )
    swap.start()
    stat_copies.append(swap)
    swap.wait_recv()
    top_v[...] = jnp.exp(top_v[...] - log_sum_exp(pair_v[...]))
    tot_v[...] = jnp.zeros_like(tot_v)

    def resp_step(i, carry):
        part = pl.ds(pl.multiple_of(i * step, step), step)
        resp = (p_v[:, part] * top_v[:, part]).astype(jnp.bfloat16)
        resp_v[:, part] = resp
        wide = resp.astype(F32)
        total = tot_v[...]
        for j in range(step // LANES):
            total += wide[:, j * LANES : (j + 1) * LANES]
        tot_v[...] = total
        return carry

    lax.fori_loop(0, nsteps, resp_step, 0)

    sent = []
    active = []
    share = out_ref.shape[0]

    def run(b):
        _, _, x_first = BLOCKS[b]
        data, h1, f1, s1, r1, h2, f2, s2, r2 = block_refs[b]
        first = (x, NX, at_x) if x_first else (z, NZ, at_z)
        second = (z, NZ, at_z) if x_first else (x, NX, at_x)
        yield from scatter("ring", *first, data, h1, f1, s1, r1, sent)
        mode = "hub" if x_first else "direct"
        yield from scatter(mode, *second, data.at[first[0]], h2, f2, s2, r2, sent)

    def run_totals():
        for k in range(NX):
            parts = [tot_v[pl.ds((j * NX + k) * share, share), :] for j in range(NZ)]
            wide = jnp.concatenate(parts, axis=0)
            own_tot_v[k] = jnp.sum(wide.T, axis=0, keepdims=True)
        copies = []

        def send(source, target, send_sem, recv_sem, device):
            copies.append(
                pltpu.make_async_remote_copy(
                    src_ref=source,
                    dst_ref=target,
                    send_sem=send_sem,
                    recv_sem=recv_sem,
                    device_id=device,
                    device_id_type=MESH,
                )
            )
            copies[-1].start()
            sent.append(copies[-1])

        for k in range(1, NX):
            to = lax.rem(x + k, NX)
            send(own_tot_v.at[to], x_tot_v.at[k], x_send.at[k], x_recv.at[k], at_x(to))
        yield
        total = own_tot_v[x]
        for k, copy in enumerate(copies):
            copy.wait_recv()
            total += x_tot_v[k + 1]
        z_tot_v[0] = total
        copies.clear()
        for k in range(1, NZ):
            to = lax.rem(z + k, NZ)
            send(z_tot_v.at[0], z_tot_v.at[k], z_send.at[k], z_recv.at[k], at_z(to))
        yield
        for copy in copies:
            copy.wait_recv()

    def put(data, x_first, first, width, value):
        for k in range(NZ):
            tile = value[k * NX * share : (k + 1) * NX * share].reshape(NX, share, width)
            if x_first:
                data[:, k, :, first : first + width] = tile
            else:
                data[k, :, :, first : first + width] = tile

    for b, (start, width, x_first) in enumerate(BLOCKS):
        data = block_refs[b][0]
        value = jnp.dot(resp_v[...], x_v[:, start : start + width], preferred_element_type=F32)
        put(data, x_first, 0, width, value)
        active.append(run(b))
        next(active[-1])
    active.append(run_totals())
    next(active[-1])
    for b in ORDER:
        next(active[b], None)
    assert all(gen.gi_frame is None for gen in active)

    own = cent_ref[pl.ds(pl.multiple_of(doc * share, share), share), :].astype(F32)
    row = jnp.sum(z_tot_v[...], axis=0)
    lane = lax.broadcasted_iota(jnp.int32, (share, LANES), 1)
    wanted = lax.broadcasted_iota(jnp.int32, (share, LANES), 0) + z * share
    total = jnp.sum(jnp.where(lane == wanted, row, 0.0), axis=1, keepdims=True) + 1.0
    for b, (start, width, x_first) in enumerate(BLOCKS):
        value = block_refs[b][0][(x, z) if x_first else (z, x)]
        out_ref[:, start : start + width] = (value + own[:, start : start + width]) / total
    for copy in stat_copies + sent:
        copy.wait_send()


def on_device(rows, centroids):
    nrows, d = rows.shape
    local = centroids.shape[0]
    ncent = lax.axis_size("cent")
    share = local // (NZ * NX)
    assert share * NZ == LANES
    scale = 1.0 / (0.6 * math.sqrt(d))
    dma = pltpu.SemaphoreType.DMA
    scratch = [
        pltpu.VMEM((nrows, d), jnp.bfloat16),
        pltpu.VMEM((local, nrows), F32),
        pltpu.VMEM((local, nrows), jnp.bfloat16),
        pltpu.VMEM((1, nrows), F32),
        pltpu.VMEM((ncent // 2, 1, nrows), F32),
        pltpu.VMEM((2, 1, nrows), F32),
        pltpu.VMEM((local, LANES), F32),
        dma((nrows // 512,)),
        dma((ncent // 2,)),
        dma((ncent // 2,)),
        pltpu.VMEM((NX, 1, LANES), F32),
        pltpu.VMEM((NX, 1, LANES), F32),
        pltpu.VMEM((NZ, 1, LANES), F32),
        dma((NX,)),
        dma((NX,)),
        dma((NZ,)),
        dma((NZ,)),
    ]
    for _, w, x_first in BLOCKS:
        n1, n2 = (NX, NZ) if x_first else (NZ, NX)
        scratch += [
            pltpu.VMEM((n1, n2, share, w), F32),
            pltpu.VMEM((2, n2 // 2, share, w), F32),
            pltpu.VMEM((2, n1 // 2 - 1, n2, share, w), F32),
            dma((2, n1 // 2)),
            dma((2, n1 // 2)),
            pltpu.VMEM((2, share // 2, w), F32),
            pltpu.VMEM((2, n2 // 2 - 1, share, w), F32),
            dma((2, n2 // 2)),
            dma((2, n2 // 2)),
        ]
    return pl.pallas_call(
        functools.partial(kernel, scale, ncent),
        out_shape=jax.ShapeDtypeStruct((share, d), F32),
        in_specs=[pl.BlockSpec(memory_space=pl.ANY), pl.BlockSpec(memory_space=pltpu.VMEM)],
        out_specs=pl.BlockSpec(memory_space=pltpu.VMEM),
        scratch_shapes=scratch,
        compiler_params=pltpu.CompilerParams(collective_id=0, has_side_effects=True),
    )(rows, centroids)


def solution(mesh):
    return jax.shard_map(
        on_device,
        mesh=mesh,
        in_specs=(P("doc", None), P("cent", None)),
        out_specs=P(("cent", "doc"), None),
        check_vma=False,
    )
```

```python
import functools
import math

import jax
import jax.numpy as jnp
from jax import lax
from jax.experimental import pallas as pl
from jax.experimental.pallas import tpu as pltpu
from jax.sharding import PartitionSpec as P

MESH = pl.DeviceIdType.MESH
F32 = jnp.float32
NZ, NX = 8, 4
LANES = 128
BLOCKS = ((0, 256, True), (256, 256, False), (512, 256, True), (768, 256, False))
ORDER = (1, 0, 3, 2, 4, 1, 3, 0, 1, 2, 3, 0, 1, 2, 3, 1, 0, 2, 3, 4)


def scatter(mode, me, n, device, data, half_in, full_in, send_sems, recv_sems, sent):
    h = data.shape[1] // 2
    last = n // 2

    def chunk_at(way, k):
        return data.at[lax.rem(me + (k if way == 0 else n - k), n)]

    def send(way, slot, source, k):
        copy = pltpu.make_async_remote_copy(
            src_ref=source,
            dst_ref=half_in.at[way] if slot == 0 else full_in.at[way, slot - 1],
            send_sem=send_sems.at[way, slot],
            recv_sem=recv_sems.at[way, slot],
            device_id=device(lax.rem(me + (k if way == 0 else n - k), n)),
            device_id_type=MESH,
        )
        copy.start()
        sent.append(copy)
        return copy

    halves = [pl.ds(0, h), pl.ds(h, h)]
    both = (0, 1)
    own = data.at[me]
    if mode == "direct":
        far = [send(w, 0, chunk_at(w, last).at[halves[w]], last) for w in both]
        near = [send(w, 1, chunk_at(w, 1), 1) for w in both]
        yield
        for w in both:
            near[w].wait_recv()
            far[w].wait_recv()
        own[...] += full_in[0, 0] + full_in[1, 0]
        for w in both:
            own[halves[w]] += half_in[w]
    elif mode == "hub":
        far = [send(w, 0, chunk_at(w, 4).at[halves[w]], 2) for w in both]
        near = [send(w, 1, chunk_at(w, 3), 1) for w in both]
        yield
        for w in both:
            near[w].wait_recv()
            far[w].wait_recv()
            hub = chunk_at(w, 2)
            hub[...] += full_in[w, 0]
            hub[halves[w]] += half_in[w]
            far[w] = send(w, 2, hub, 2)
        near = [send(w, 3, chunk_at(w, 1), 1) for w in both]
        yield
        for w in both:
            near[w].wait_recv()
            far[w].wait_recv()
        own[...] += (full_in[0, 1] + full_in[0, 2]) + (full_in[1, 1] + full_in[1, 2])
    else:
        copies = [None, None]
        for slot in range(last):
            for w in both:
                chunk = chunk_at(w, last - slot)
                if slot == 0:
                    copies[w] = send(w, 0, chunk.at[halves[w]], 1)
                    continue
                copies[w].wait_recv()
                if slot == 1:
                    chunk[halves[w]] += half_in[w]
                else:
                    chunk[...] += full_in[w, slot - 2]
                copies[w] = send(w, slot, chunk, 1)
            yield
        for w in both:
            copies[w].wait_recv()
        own[...] += full_in[0, last - 2] + full_in[1, last - 2]


def kernel(scale, ncent, *refs):
    rows_hbm, cent_hbm, out_ref, cent_ref, x_v, p_v, resp_v, top_v, stat_v, pair_v, tot_v = refs[:11]
    own_tot_v, x_tot_v, z_tot_v, x_send, x_recv, z_send, z_recv = refs[14:21]
    in_sems, stat_send, stat_recv = refs[11:14]
    block_refs = [refs[21 + 9 * b : 30 + 9 * b] for b in range(len(BLOCKS))]
    rows, step = x_v.shape[0], 512
    nsteps = rows // step
    doc, cent = lax.axis_index("doc"), lax.axis_index("cent")
    z, x = doc // NX, lax.rem(doc, NX)

    def chunk_in(i):
        part = pl.ds(i * step, step)
        return pltpu.make_async_copy(rows_hbm.at[part], x_v.at[part], in_sems.at[i])

    cent_in = pltpu.make_async_copy(cent_hbm, cent_ref, in_sems.at[nsteps])
    cent_in.start()
    for i in range(nsteps):
        chunk_in(i).start()

    def at_z(k):
        return {"doc": k * NX + x}

    def at_x(k):
        return {"doc": z * NX + k}

    barrier = pltpu.get_barrier_semaphore()
    near = [at_z(lax.rem(z + k, NZ)) for k in range(1, NZ)]
    near += [at_x(lax.rem(x + k, NX)) for k in range(1, NX)]
    near += [{"cent": lax.rem(cent + k, ncent)} for k in range(2, ncent, 2)]
    partner = {"cent": cent + 1 - 2 * lax.rem(cent, 2)}
    near.append(partner)
    for other in near:
        pl.semaphore_signal(barrier, inc=1, device_id=other, device_id_type=MESH)

    def logits_of(i):
        chunk_in(i).wait()
        return lax.dot_general(
            cent_ref[...],
            x_v[i * step : (i + 1) * step, :],
            (((1,), (1,)), ((), ())),
            preferred_element_type=F32,
        )

    cent_in.wait()
    product = logits_of(0)
    for i in range(nsteps):
        following = logits_of(i + 1) if i + 1 < nsteps else None
        part = slice(i * step, (i + 1) * step)
        logits = product * scale
        top = jnp.max(logits, axis=0, keepdims=True)
        p = jnp.exp(logits - top)
        p_v[:, part] = p
        top_v[:, part] = top
        stat_v[0, :, part] = top + jnp.log(jnp.sum(p, axis=0, keepdims=True))
        product = following
    pl.semaphore_wait(barrier, len(near))

    def log_sum_exp(values):
        highest = jnp.max(values, axis=0)
        return highest + jnp.log(jnp.sum(jnp.exp(values - highest[None]), axis=0))

    chips = ncent // 2
    stat_copies = []
    for k in sorted(range(1, chips), key=lambda k: -min(k, chips - k)):
        stat_copies.append(
            pltpu.make_async_remote_copy(
                src_ref=stat_v.at[0],
                dst_ref=stat_v.at[k],
                send_sem=stat_send.at[k],
                recv_sem=stat_recv.at[k],
                device_id={"cent": lax.rem(cent + 2 * k, ncent)},
                device_id_type=MESH,
            )
        )
        stat_copies[-1].start()
    for copy in stat_copies:
        copy.wait_recv()
    pair_v[0] = log_sum_exp(stat_v[...])
    swap = pltpu.make_async_remote_copy(
        src_ref=pair_v.at[0],
        dst_ref=pair_v.at[1],
        send_sem=stat_send.at[0],
        recv_sem=stat_recv.at[0],
        device_id=partner,
        device_id_type=MESH,
    )
    swap.start()
    stat_copies.append(swap)
    swap.wait_recv()
    top_v[...] = jnp.exp(top_v[...] - log_sum_exp(pair_v[...]))
    total = jnp.zeros(tot_v.shape, F32)
    for i in range(nsteps):
        part = slice(i * step, (i + 1) * step)
        resp = (p_v[:, part] * top_v[:, part]).astype(jnp.bfloat16)
        resp_v[:, part] = resp
        wide = resp.astype(F32)
        for j in range(step // LANES):
            total += wide[:, j * LANES : (j + 1) * LANES]
    tot_v[...] = total

    sent = []
    active = []
    share = out_ref.shape[0]

    def run(b):
        _, _, x_first = BLOCKS[b]
        data, h1, f1, s1, r1, h2, f2, s2, r2 = block_refs[b]
        first = (x, NX, at_x) if x_first else (z, NZ, at_z)
        second = (z, NZ, at_z) if x_first else (x, NX, at_x)
        yield from scatter("ring", *first, data, h1, f1, s1, r1, sent)
        mode = "hub" if x_first else "direct"
        yield from scatter(mode, *second, data.at[first[0]], h2, f2, s2, r2, sent)

    def run_totals():
        for k in range(NX):
            parts = [tot_v[pl.ds((j * NX + k) * share, share), :] for j in range(NZ)]
            wide = jnp.concatenate(parts, axis=0)
            own_tot_v[k] = jnp.sum(wide.T, axis=0, keepdims=True)
        copies = []

        def send(source, target, send_sem, recv_sem, device):
            copies.append(
                pltpu.make_async_remote_copy(
                    src_ref=source,
                    dst_ref=target,
                    send_sem=send_sem,
                    recv_sem=recv_sem,
                    device_id=device,
                    device_id_type=MESH,
                )
            )
            copies[-1].start()
            sent.append(copies[-1])

        for k in range(1, NX):
            to = lax.rem(x + k, NX)
            send(own_tot_v.at[to], x_tot_v.at[k], x_send.at[k], x_recv.at[k], at_x(to))
        yield
        total = own_tot_v[x]
        for k, copy in enumerate(copies):
            copy.wait_recv()
            total += x_tot_v[k + 1]
        z_tot_v[0] = total
        copies.clear()
        for k in range(1, NZ):
            to = lax.rem(z + k, NZ)
            send(z_tot_v.at[0], z_tot_v.at[k], z_send.at[k], z_recv.at[k], at_z(to))
        yield
        for copy in copies:
            copy.wait_recv()

    def put(data, x_first, first, width, value):
        for k in range(NZ):
            tile = value[k * NX * share : (k + 1) * NX * share].reshape(NX, share, width)
            if x_first:
                data[:, k, :, first : first + width] = tile
            else:
                data[k, :, :, first : first + width] = tile

    for b, (start, width, x_first) in enumerate(BLOCKS):
        data = block_refs[b][0]
        value = jnp.dot(resp_v[...], x_v[:, start : start + width], preferred_element_type=F32)
        put(data, x_first, 0, width, value)
        active.append(run(b))
        next(active[-1])
    active.append(run_totals())
    next(active[-1])
    for b in ORDER:
        next(active[b], None)
    assert all(gen.gi_frame is None for gen in active)

    own = cent_ref[pl.ds(pl.multiple_of(doc * share, share), share), :].astype(F32)
    row = jnp.sum(z_tot_v[...], axis=0)
    lane = lax.broadcasted_iota(jnp.int32, (share, LANES), 1)
    wanted = lax.broadcasted_iota(jnp.int32, (share, LANES), 0) + z * share
    total = jnp.sum(jnp.where(lane == wanted, row, 0.0), axis=1, keepdims=True) + 1.0
    for b, (start, width, x_first) in enumerate(BLOCKS):
        value = block_refs[b][0][(x, z) if x_first else (z, x)]
        out_ref[:, start : start + width] = (value + own[:, start : start + width]) / total
    for copy in stat_copies + sent:
        copy.wait_send()


def on_device(rows, centroids):
    nrows, d = rows.shape
    local = centroids.shape[0]
    ncent = lax.axis_size("cent")
    share = local // (NZ * NX)
    assert share * NZ == LANES
    scale = 1.0 / (0.6 * math.sqrt(d))
    dma = pltpu.SemaphoreType.DMA
    scratch = [
        pltpu.VMEM((local, d), jnp.bfloat16),
        pltpu.VMEM((nrows, d), jnp.bfloat16),
        pltpu.VMEM((local, nrows), F32),
        pltpu.VMEM((local, nrows), jnp.bfloat16),
        pltpu.VMEM((1, nrows), F32),
        pltpu.VMEM((ncent // 2, 1, nrows), F32),
        pltpu.VMEM((2, 1, nrows), F32),
        pltpu.VMEM((local, LANES), F32),
        dma((nrows // 512 + 1,)),
        dma((ncent // 2,)),
        dma((ncent // 2,)),
        pltpu.VMEM((NX, 1, LANES), F32),
        pltpu.VMEM((NX, 1, LANES), F32),
        pltpu.VMEM((NZ, 1, LANES), F32),
        dma((NX,)),
        dma((NX,)),
        dma((NZ,)),
        dma((NZ,)),
    ]
    for _, w, x_first in BLOCKS:
        n1, n2 = (NX, NZ) if x_first else (NZ, NX)
        scratch += [
            pltpu.VMEM((n1, n2, share, w), F32),
            pltpu.VMEM((2, n2 // 2, share, w), F32),
            pltpu.VMEM((2, n1 // 2 - 1, n2, share, w), F32),
            dma((2, n1 // 2)),
            dma((2, n1 // 2)),
            pltpu.VMEM((2, share // 2, w), F32),
            pltpu.VMEM((2, n2 // 2 - 1, share, w), F32),
            dma((2, n2 // 2)),
            dma((2, n2 // 2)),
        ]
    return pl.pallas_call(
        functools.partial(kernel, scale, ncent),
        out_shape=jax.ShapeDtypeStruct((share, d), F32),
        in_specs=[pl.BlockSpec(memory_space=pl.ANY)] * 2,
        out_specs=pl.BlockSpec(memory_space=pltpu.VMEM),
        scratch_shapes=scratch,
        compiler_params=pltpu.CompilerParams(collective_id=0, has_side_effects=True),
    )(rows, centroids)


def solution(mesh):
    return jax.shard_map(
        on_device,
        mesh=mesh,
        in_specs=(P("doc", None), P("cent", None)),
        out_specs=P(("cent", "doc"), None),
        check_vma=False,
    )
```
